128 devices in a mesh: blk: 32 (over x, y_hi, z), grp: 4 (over y_lo, core).
Axes of the slice: x: 4, y: 4 (y_hi: 2, y_lo: 2; y = y_hi * 2 + y_lo), z: 4, core: 2. Of those that a mesh axis runs over, the one named last changes fastest.
Arguments:
- amplitudes: bfloat16 [1920, 1920], P('blk'), may hold values from -6 to 6
- hole_panel: bfloat16 [1920, 32, 1920], P(None, 'blk', 'grp'), may hold values from -0.375 to 0.375
- virt_fock: bfloat16 [1920, 1920], replicated, may hold values from -0.125 to 0.125
- irrep_sizes: int32 [8], replicated, may hold values from 1 to 480, 1920 in all
- pair_irreps: int32 [32], P('blk'), may hold values from 0 to 7
Outputs:
- dressed: bfloat16 [1920, 32, 1920], P('grp', 'blk')
The draws below stay inside these ranges and needn't reach their ends.
Inputs may be any that keep to these rules, and one draw needn't show every extreme that they name: `irrep_sizes`: the 8 entries sum to 1920.
All inputs are finite; a program needn't handle non-finite values.
Results may differ from the reference program's by a relative error of at most 0.0049.
Values may be sent and summed in bfloat16 or wider, within the bound.
A program may use at most 128 MiB of HBM per device.

```python
import math
import jax
import jax.numpy as jnp
import numpy as np
from jax import lax

NVIR = 1920
NIRREP = 8
OCC_SLAB = 32


def with_ends(values, key, least, top_value):
    longest = values.shape.index(max(values.shape))
    spots = []
    for shift in (0, 1):
        where = [jax.random.randint(jax.random.fold_in(key, axis), (), 0, length) for axis, length in enumerate(values.shape)]
        where[longest] = (where[longest] + shift) % values.shape[longest]
        spots.append(tuple(where))
    return values.at[spots[0]].set(least).at[spots[1]].set(top_value)


def block_scale(rng, dims, pieces, low, largest):
    loudness, own = 1.0, jax.random.fold_in(rng, 6)
    for position, shards_of in pieces:
        steps = jnp.exp(jax.random.uniform(jax.random.fold_in(own, position), (shards_of,), jnp.float32, low / len(pieces), largest / len(pieces)))
        loudness = loudness * jnp.repeat(steps, dims[position] // shards_of).reshape([-1 if axis == position else 1 for axis in range(len(dims))])
    return loudness


def length_profile(number_of, total, limit, lean):
    weights = [(1 << 20) // math.isqrt(rank ** lean) + 1 for rank in range(2, number_of + 1)]
    spare, counts = total - limit - (number_of - 1), [1] * (number_of - 1)
    while spare > 0:
        candidates = [i for i in range(number_of - 1) if counts[i] < limit]
        mass, left = sum([weights[i] for i in candidates]), spare
        for i in candidates:
            more = min(limit - counts[i], max(1, left * weights[i] // mass), spare)
            counts[i] = counts[i] + more
            spare = spare - more
    return np.array([limit] + counts)


def ragged_sizes(stream_key, count, total, bound, skew):
    if count == 2:
        one = jax.random.randint(stream_key, (), max(1, total - bound), min(bound, total - 1) + 1)
        return jnp.stack([one, total - one])
    tallies = jnp.asarray(length_profile(count, total, bound, skew), jnp.int32)
    pairs = (count - 1) // 2
    source_of, taker = tallies[1:1 + 2 * pairs:2], tallies[2:2 + 2 * pairs:2]
    slack = jnp.minimum(source_of - 1, bound - taker)
    shifted = jax.random.randint(jax.random.fold_in(stream_key, 1), (pairs,), 0, 1 << 20) % (slack + 1)
    tallies = tallies.at[1:1 + 2 * pairs:2].set(source_of - shifted).at[2:2 + 2 * pairs:2].set(taker + shifted)
    return tallies[jax.random.permutation(jax.random.fold_in(stream_key, 2), count)]


def normal_values(key, dims, scale, bound, cuts=(), kind=jnp.bfloat16):
    factor_of = block_scale(key, dims, cuts, -0.22, 0.18) if cuts else 1.0
    result = jax.random.normal(key, dims, jnp.float32) * scale * factor_of
    return jnp.minimum(jnp.maximum(result, -bound), bound).astype(kind)


def setup_inputs(seed: int = 0) -> dict:
    arg_keys = jax.random.split(jax.random.key(seed), 6)
    amplitudes = normal_values(arg_keys[0], (NVIR, NVIR), 1.0, 6.0, ((0, 32),))
    hole_panel = normal_values(arg_keys[1], (NVIR, OCC_SLAB, NVIR), (NVIR // 8) ** -0.5, 0.375, ((1, 32), (2, 4)))
    virt_fock = normal_values(arg_keys[2], (NVIR, NVIR), NVIR ** -0.5, 0.125)
    irrep_sizes = ragged_sizes(arg_keys[3], NIRREP, NVIR, NVIR // 4, 1).astype(jnp.int32)
    pair_irreps = with_ends(jax.random.randint(arg_keys[4], (OCC_SLAB,), 0, 8), jax.random.fold_in(arg_keys[4], 1), 0, 7).astype(jnp.int32)
    return {"amplitudes": amplitudes, "hole_panel": hole_panel, "virt_fock": virt_fock, "irrep_sizes": irrep_sizes, "pair_irreps": pair_irreps}


def irrep_of(positions, block_sizes):
    bounds = jnp.cumsum(block_sizes)[:-1]
    return jnp.sum((positions[:, None] >= bounds[None, :]).astype(jnp.int32), axis=1)


def reference(amplitudes, hole_panel, virt_fock, irrep_sizes, pair_irreps):
    positions = jnp.arange(NVIR, dtype=jnp.int32)
    labels = irrep_of(positions, irrep_sizes)
    pair_xor = jnp.bitwise_xor(labels[:, None], labels[None, :])

    def one_pair(pair_item):
        pair_panel, target = pair_item
        masked = jnp.where(pair_xor == target, pair_panel, jnp.zeros((), pair_panel.dtype))
        coupled = jnp.dot(amplitudes, masked, preferred_element_type=jnp.float32).astype(jnp.bfloat16)
        return jnp.dot(coupled, virt_fock, preferred_element_type=jnp.float32).astype(jnp.bfloat16)

    stacked = lax.map(one_pair, (jnp.moveaxis(hole_panel, 1, 0), pair_irreps))
    return jnp.moveaxis(stacked, 0, 1)
```

```python
import jax
import jax.numpy as jnp
from jax import lax
from jax.sharding import PartitionSpec as P


def irrep_of(positions, block_sizes):
    bounds = jnp.cumsum(block_sizes)[:-1]
    return jnp.sum((positions[:, None] >= bounds[None, :]).astype(jnp.int32), axis=1)


def make_local(n_blk, n_grp):
    def local(amplitudes, hole_panel, virt_fock, irrep_sizes, pair_irreps):
        rows = amplitudes.shape[0]
        virtuals = amplitudes.shape[1]
        quarter = hole_panel.shape[2]
        g = lax.axis_index("grp")
        piece = rows // n_grp
        per = n_blk // n_grp
        perm = []
        for q in range(n_grp):
            for k in range(per):
                for i in range(n_grp):
                    perm.append(((per * q + k) * n_grp + i, (n_grp * k + i) * n_grp + q))
        mine = lax.dynamic_slice_in_dim(amplitudes, g * piece, piece, 0)
        mine = lax.ppermute(mine, ("blk", "grp"), perm)
        t_rows = lax.all_gather(mine, "blk", axis=0, tiled=True)
        labels = irrep_of(jnp.arange(virtuals, dtype=jnp.int32), irrep_sizes)
        panel = lax.all_gather(hole_panel.reshape(virtuals, quarter), "grp", axis=1, tiled=True)
        allowed = jnp.bitwise_xor(labels[:, None], labels[None, :]) == pair_irreps[0]
        masked = jnp.where(allowed, panel, jnp.zeros((), jnp.bfloat16))
        coupled = jnp.dot(t_rows, masked, preferred_element_type=jnp.float32).astype(jnp.bfloat16)
        out = jnp.dot(coupled, virt_fock, preferred_element_type=jnp.float32).astype(jnp.bfloat16)
        return out.reshape(quarter, 1, virtuals)

    return local


def solution(mesh):
    in_specs = (P("blk", None), P(None, "blk", "grp"), P(), P(), P("blk"))
    out_specs = P("grp", "blk", None)
    local = make_local(mesh.shape["blk"], mesh.shape["grp"])
    return jax.shard_map(local, mesh=mesh, in_specs=in_specs, out_specs=out_specs, check_vma=False)
```

```python
import functools

import jax
import jax.numpy as jnp
from jax import lax
from jax.experimental import pallas as pl
from jax.experimental.pallas import tpu as pltpu
from jax.sharding import PartitionSpec as P

MESH = pl.DeviceIdType.MESH
F32, BF16 = jnp.float32, jnp.bfloat16
N = 1920
QR = 480
NB, NG = 32, 4
ROWS = 60
PAD = 64
WIN = 640
NT = N // 16
NW = (N - WIN) // 128 + 1
SPLIT = ((0, 512), (512, 512), (1024, 512), (1536, 384))
CH = 3
CR = QR // CH


def kernel(amp, wt, fock, sizes, pair, out,
           amp64, tbuf, cbuf, mfull, fbuf, coupled,
           scat_s, scat_r, ag_s, ag_r, pan_s, pan_r, f_sem):
    blk, g = lax.axis_index("blk"), lax.axis_index("grp")
    x, yh, z = blk // 8, (blk // 4) % 2, blk % 4
    yl, c = g // 2, g % 2

    def dev(x_, yh_, z_, yl_, c_):
        return (x_ * 8 + yh_ * 4 + z_, yl_ * 2 + c_)

    q = g
    d = (x - q + 4) % 4
    rel = d // 2
    src_c = (1 - rel) * ((c + 1 + d) % 2) + rel * (d - 2 + 2) % 2
    source = dev(q, (yh + rel) % 2, z, (yl + rel) % 2, src_c)
    tyl, tc = x // 2, x % 2
    trel = (yl + tyl) % 2
    td = (1 - trel) * (1 - (c + tc) % 2) + trel * (2 + c)
    target = dev((x + td) % 4, (yh + trel) % 2, z, tyl, tc)
    sibling = dev(x, yh, z, yl, 1 - c)
    other = dev(x, yh, z, 1 - yl, c)

    def plane(sx, sz):
        return dev((x + sx) % 4, yh, (z + sz) % 4, yl, c)

    bar = pltpu.get_barrier_semaphore()
    peers = [plane(s, 0) for s in (1, 2, 3)] + [plane(0, s) for s in (1, 2, 3)]
    for to in peers + [sibling, other, source]:
        pl.semaphore_signal(bar, inc=1, device_id=to, device_id_type=MESH)
    fcopy = pltpu.make_async_copy(fock, fbuf, f_sem)
    fcopy.start()
    amp64[pl.ds(0, ROWS), :] = amp[...]
    amp64[pl.ds(ROWS, PAD - ROWS), :] = jnp.zeros((PAD - ROWS, N), BF16)
    pl.semaphore_wait(bar, len(peers) + 3)

    pending = []

    th = ((td + 1) // 2) % 2
    for cl in range(2):
        col = pl.multiple_of(th * 896 + cl * 512, 128)
        copy = pltpu.make_async_remote_copy(
            amp64.at[:, pl.ds(col, 512)], tbuf.at[th * 2 + cl, yh * 4 + z],
            scat_s.at[cl], scat_r.at[cl], device_id=target, device_id_type=MESH)
        copy.start()
        pending.append(copy)

    p = pair[0]
    run = jnp.int32(0)
    bound = []
    for r in range(8):
        bound.append(run)
        run = run + sizes[r]
    bound.append(run)
    lo, hi, win = [], [], []
    for r in range(8):
        s = jnp.bitwise_xor(jnp.int32(r), p)
        first_lane, end_lane = jnp.int32(0), jnp.int32(0)
        for i in range(8):
            first_lane = jnp.where(s == i, bound[i], first_lane)
            end_lane = jnp.where(s == i, bound[i + 1], end_lane)
        lo.append(first_lane)
        hi.append(end_lane)
        win.append(jnp.minimum(jnp.right_shift(first_lane, 7), NW - 1))
    left_of = [lo[r] - win[r] * 128 for r in range(8)]
    right_of = [hi[r] - win[r] * 128 for r in range(8)]

    base = g * QR

    def pan_copy(kind, i, owner, to):
        rows = cbuf.at[pl.ds(pl.multiple_of(owner * QR + i * CR, 16), CR), :]
        return pltpu.make_async_remote_copy(
            rows, rows, pan_s.at[kind, i], pan_r.at[kind, i], device_id=to, device_id_type=MESH)

    lane = lax.broadcasted_iota(jnp.int32, (16, 128), 1)
    sub = lax.broadcasted_iota(jnp.int32, (16, 128), 0)

    def of_row(b, values):
        pick = jnp.full((16, 128), values[0])
        for r in range(1, 8):
            pick = jnp.where(b >= bound[r], values[r], pick)
        return pick

    def masks(b):
        w = of_row(b, win).astype(F32).astype(BF16)
        return [w == jnp.asarray(v, BF16) for v in range(NW)]

    def compact(t, _):
        row = pl.multiple_of(t * 16, 16)
        b = sub + (base + row)
        at = masks(b)
        left, right = of_row(b, left_of), of_row(b, right_of)
        for j in range(WIN // 128):
            acc = wt[pl.ds(row, 16), pl.ds(j * 128, 128)]
            for v in range(1, NW):
                acc = jnp.where(at[v], wt[pl.ds(row, 16), pl.ds((v + j) * 128, 128)], acc)
            keep = (lane + j * 128 >= left) & (lane + j * 128 < right)
            acc = jnp.where(keep, acc.astype(F32), 0.0).astype(BF16)
            cbuf[pl.ds(pl.multiple_of(base + row, 16), 16), pl.ds(j * 128, 128)] = acc
        return 0

    for i in range(CH):
        lax.fori_loop(i * (CR // 16), (i + 1) * (CR // 16), compact, 0)
        for kind, to in ((0, other), (1, sibling)):
            copy = pan_copy(kind, i, g, to)
            copy.start()
            pending.append(copy)

    def slot(dx, dz, cl):
        xo, zo = (x - dx + 4) % 4, (z - dz + 4) % 4
        do = (xo - q + 4) % 4
        return tbuf.at[(((do + 1) // 2) % 2) * 2 + cl, ((yh + do // 2) % 2) * 4 + zo]

    count = [0, 0]

    def axes(cl, a, b):
        return (a, b) if cl == 0 else (b, a)

    def send(cl, a, b, sa, sb):
        dx, dz = axes(cl, a, b)
        sx, sz = axes(cl, sa, sb)
        there = cl * 16 + ((a + sa) % 4) * 4 + (b + sb) % 4
        where = slot(dx, dz, cl)
        copy = pltpu.make_async_remote_copy(
            where, where, ag_s.at[cl * 16 + count[cl]], ag_r.at[there],
            device_id=plane(sx, sz), device_id_type=MESH)
        count[cl] += 1
        copy.start()
        pending.append(copy)

    def arrived(cl, a, b):
        dx, dz = axes(cl, a, b)
        where = slot(dx, dz, cl)
        pltpu.make_async_remote_copy(
            where, where, ag_s.at[cl * 16 + 15], ag_r.at[cl * 16 + a * 4 + b],
            device_id=sibling, device_id_type=MESH).wait_recv()

    for cl in range(2):
        where = slot(0, 0, cl)
        pltpu.make_async_remote_copy(
            where, where, scat_s.at[cl], scat_r.at[cl], device_id=sibling, device_id_type=MESH).wait_recv()
        for s in (1, 3, 2):
            send(cl, 0, 0, s, 0)
        send(cl, 0, 0, 0, 1)
        send(cl, 0, 0, 0, 3)
    for a in (1, 3, 2):
        for cl in range(2):
            arrived(cl, a, 0)
            send(cl, a, 0, 0, 1)
            send(cl, a, 0, 0, 3)
    for a, b in ((0, 1), (3, 3), (1, 1), (2, 3)):
        for cl in range(2):
            arrived(cl, a, b)
            send(cl, a, b, 0, b)

    for i in range(CH):
        pan_copy(0, i, (1 - yl) * 2 + c, sibling).wait_recv()
        copy = pan_copy(2, i, (1 - yl) * 2 + c, sibling)
        copy.start()
        pending.append(copy)
    for i in range(CH):
        pan_copy(1, i, yl * 2 + 1 - c, sibling).wait_recv()
        pan_copy(2, i, (1 - yl) * 2 + 1 - c, sibling).wait_recv()

    def expand(t, _):
        row = pl.multiple_of(t * 16, 16)
        at = masks(sub + row)
        part = [cbuf[pl.ds(row, 16), pl.ds(j * 128, 128)] for j in range(WIN // 128)]
        for k in range(N // 128):
            acc = jnp.zeros((16, 128), BF16)
            for j in range(WIN // 128):
                if 0 <= k - j < NW:
                    acc = jnp.where(at[k - j], part[j], acc)
            mfull[pl.ds(row, 16), pl.ds(k * 128, 128)] = acc
        return 0

    lax.fori_loop(0, NT, expand, 0)
    fcopy.wait()

    for cl in range(2):
        for a in range(4):
            for b in (1, 2, 3):
                if (a, b) not in ((0, 1), (3, 3), (1, 1), (2, 3)):
                    arrived(cl, a, b)
    for copy in pending:
        copy.wait_send()

    for col, width in SPLIT:
        acc = jnp.zeros((8 * PAD, width), F32)
        for ci, off, at in ((0, 0, 0), (1, 0, 512), (2, 128, 1024), (3, 0, 1408)):
            lhs = tbuf[ci].reshape(8 * PAD, 512)[:, off:]
            acc = acc + lax.dot_general(
                lhs, mfull[pl.ds(col, width), pl.ds(at, 512 - off)],
                (((1,), (1,)), ((), ())), preferred_element_type=F32)
        coupled[:, pl.ds(col, width)] = acc.astype(BF16)

    for col, width in SPLIT:
        acc = jnp.dot(coupled[...], fbuf[:, pl.ds(col, width)], preferred_element_type=F32)
        for k in range(8):
            out[pl.ds(k * ROWS, ROWS), pl.ds(col, width)] = acc[k * PAD:k * PAD + ROWS].astype(BF16)


def local(amplitudes, hole_panel, virt_fock, irrep_sizes, pair_irreps):
    wt = jnp.transpose(hole_panel.reshape(N, QR))
    vmem = pl.BlockSpec(memory_space=pltpu.VMEM)
    smem = pl.BlockSpec(memory_space=pltpu.SMEM)
    out = pl.pallas_call(
        kernel,
        out_shape=jax.ShapeDtypeStruct((QR, N), BF16),
        in_specs=[vmem, vmem, pl.BlockSpec(memory_space=pl.ANY), smem, smem],
        out_specs=vmem,
        scratch_shapes=[
            pltpu.VMEM((PAD, N), BF16),
            pltpu.VMEM((4, 8, PAD, 512), BF16),
            pltpu.VMEM((N, WIN), BF16),
            pltpu.VMEM((N, N), BF16),
            pltpu.VMEM((N, N), BF16),
            pltpu.VMEM((8 * PAD, N), BF16),
            pltpu.SemaphoreType.DMA((2,)),
            pltpu.SemaphoreType.DMA((2,)),
            pltpu.SemaphoreType.DMA((32,)),
            pltpu.SemaphoreType.DMA((32,)),
            pltpu.SemaphoreType.DMA((3, CH)),
            pltpu.SemaphoreType.DMA((3, CH)),
            pltpu.SemaphoreType.DMA,
        ],
        compiler_params=pltpu.CompilerParams(
            collective_id=0, has_side_effects=True, vmem_limit_bytes=50 << 20),
    )(amplitudes, wt, virt_fock, irrep_sizes, pair_irreps)
    return out.reshape(QR, 1, N)


def solution(mesh):
    in_specs = (P("blk", None), P(None, "blk", "grp"), P(), P(), P("blk"))
    out_specs = P("grp", "blk", None)
    return jax.shard_map(local, mesh=mesh, in_specs=in_specs, out_specs=out_specs, check_vma=False)
```

```python
import functools

import jax
import jax.numpy as jnp
from jax import lax
from jax.experimental import pallas as pl
from jax.experimental.pallas import tpu as pltpu
from jax.sharding import PartitionSpec as P

MESH = pl.DeviceIdType.MESH
F32, BF16 = jnp.float32, jnp.bfloat16
N = 1920
QR = 480
NB, NG = 32, 4
ROWS = 60
PAD = 64
WIN = 640
NW = (N - WIN) // 128 + 1
FWIN = 496
NF = (WIN - FWIN) // 16 + 1
SPLIT = ((0, 512), (512, 512), (1024, 512), (1536, 384))
CC = 384
CH = 4


def kernel(amp, wt, fock, sizes, pair, out,
           amp64, tbuf, cbuf, ctb, cts, mfull, fall, coupled,
           a_s, a_r, b_s, b_r, pan_s, pan_r, f_sem):
    blk, g = lax.axis_index("blk"), lax.axis_index("grp")
    x, yh, z = blk // 8, (blk // 4) % 2, blk % 4
    yl, c = g // 2, g % 2

    def dev(x_, yh_, z_, yl_, c_):
        return (x_ * 8 + yh_ * 4 + z_, yl_ * 2 + c_)

    q = g
    d = (x - q + 4) % 4
    a_use = ((d + 3) % 4) // 2
    a_core = (a_use + c) % 2
    b_rel = d // 2
    b_core = (1 - b_rel) * ((c + 1 + d) % 2) + b_rel * ((d + 2) % 4)
    sources = [dev(q, yh, z, yl, a_core), dev(q, 1 - yh, z, 1 - yl, a_use),
               dev(q, (yh + b_rel) % 2, z, (yl + b_rel) % 2, b_core)]
    tyl, tc = x // 2, x % 2
    trel = (yl + tyl) % 2
    use = (1 - trel) * ((c + tc) % 2) + trel * c
    a_targets = [dev((x + 1 + 2 * use + i) % 4, (yh + trel) % 2, z, tyl, tc) for i in range(2)]
    td = (1 - trel) * (1 - (c + tc) % 2) + trel * (2 + c)
    b_target = dev((x + td) % 4, (yh + trel) % 2, z, tyl, tc)
    sibling = dev(x, yh, z, yl, 1 - c)
    other = dev(x, yh, z, 1 - yl, c)

    def plane(sx, sz):
        return dev((x + sx) % 4, yh, (z + sz) % 4, yl, c)

    bar = pltpu.get_barrier_semaphore()
    peers = [plane(s, 0) for s in (1, 2, 3)] + [plane(0, s) for s in (1, 2, 3)]
    for to in peers + sources + [sibling, other]:
        pl.semaphore_signal(bar, inc=1, device_id=to, device_id_type=MESH)
    far0 = (1 - yl) * 2
    fcopies = []
    for slot in range(4):
        owner = (yl * 2 + slot) % 4
        fcopies.append(pltpu.make_async_copy(
            fock.at[pl.ds(pl.multiple_of(owner * QR, 16), QR)],
            fall.at[pl.ds(slot * 512, QR)], f_sem.at[slot]))
    for copy in fcopies:
        copy.start()
    for slot in range(4):
        fall[pl.ds(slot * 512 + QR, 32), :] = jnp.zeros((32, N), BF16)
    amp64[pl.ds(0, ROWS), :] = amp[...]
    amp64[pl.ds(ROWS, PAD - ROWS), :] = jnp.zeros((PAD - ROWS, N), BF16)

    p = pair[0]
    run = jnp.int32(0)
    bound = []
    for r in range(8):
        bound.append(run)
        run = run + sizes[r]
    bound.append(run)
    lo, hi, win = [], [], []
    for r in range(8):
        s = jnp.bitwise_xor(jnp.int32(r), p)
        first_lane, end_lane = jnp.int32(0), jnp.int32(0)
        for i in range(8):
            first_lane = jnp.where(s == i, bound[i], first_lane)
            end_lane = jnp.where(s == i, bound[i + 1], end_lane)
        lo.append(first_lane)
        hi.append(end_lane)
        win.append(jnp.minimum(jnp.right_shift(first_lane, 7), NW - 1))
    fine = [jnp.minimum(jnp.right_shift(lo[r], 4), (N - FWIN) // 16) - win[r] * 8 for r in range(8)]
    left_of = [lo[r] - win[r] * 128 for r in range(8)]
    right_of = [hi[r] - win[r] * 128 for r in range(8)]

    base = g * QR

    def pan_copy(kind, i, owner, to):
        part = (ctb if kind == 1 else cts).at[owner, i]
        return pltpu.make_async_remote_copy(
            part, part, pan_s.at[kind, i], pan_r.at[kind, i], device_id=to, device_id_type=MESH)

    lane = lax.broadcasted_iota(jnp.int32, (16, 128), 1)
    sub = lax.broadcasted_iota(jnp.int32, (16, 128), 0)

    def of_row(b, values):
        pick = jnp.full((16, 128), values[0])
        for r in range(1, 8):
            pick = jnp.where(b >= bound[r], values[r], pick)
        return pick

    def masks(b):
        w = of_row(b, win).astype(F32).astype(BF16)
        return [w == jnp.asarray(v, BF16) for v in range(NW)]

    def compact(t, _):
        row = pl.multiple_of(t * 16, 16)
        b = sub + (base + row)
        at = masks(b)
        left, right = of_row(b, left_of), of_row(b, right_of)
        for j in range(WIN // 128):
            acc = wt[pl.ds(row, 16), pl.ds(j * 128, 128)]
            for v in range(1, NW):
                acc = jnp.where(at[v], wt[pl.ds(row, 16), pl.ds((v + j) * 128, 128)], acc)
            keep = (lane + j * 128 >= left) & (lane + j * 128 < right)
            acc = jnp.where(keep, acc.astype(F32), 0.0).astype(BF16)
            cbuf[pl.ds(row, 16), pl.ds(j * 128, 128)] = acc
        return 0

    lax.fori_loop(0, QR // 16, compact, 0)
    cbuf[pl.ds(QR, 32), :] = jnp.zeros((32, WIN), BF16)
    for i in range(CH):
        ctb[g, i] = jnp.transpose(cbuf[pl.ds(i * 128, 128), :])

    def fine_masks(owner, i):
        f = of_row(lane + (owner * QR + i * 128), fine).astype(F32).astype(BF16)
        return [f == jnp.asarray(v, BF16) for v in range(NF)]

    def narrow(i, _):
        at = fine_masks(g, i)
        for u in range(FWIN // 16):
            acc = ctb[g, i, pl.ds(u * 16, 16), :]
            for v in range(1, NF):
                acc = jnp.where(at[v], ctb[g, i, pl.ds((u + v) * 16, 16), :], acc)
            cts[g, i, pl.ds(u * 16, 16), :] = acc
        return 0

    def widen(owner, i):
        at = fine_masks(owner, i)
        for u in range(WIN // 16):
            acc = jnp.zeros((16, 128), BF16)
            for v in range(NF):
                if 0 <= u - v < FWIN // 16:
                    acc = jnp.where(at[v], cts[owner, i, pl.ds((u - v) * 16, 16), :], acc)
            ctb[owner, i, pl.ds(u * 16, 16), :] = acc

    lax.fori_loop(0, CH, narrow, 0)
    pl.semaphore_wait(bar, len(peers) + 5)

    pending = []

    def push(copy):
        copy.start()
        pending.append(copy)

    def columns(chunk):
        return pl.ds(pl.multiple_of(chunk * CC, 128), CC)

    def remote(src, dst, s_sem, r_sem, to):
        return pltpu.make_async_remote_copy(src, dst, s_sem, r_sem, device_id=to, device_id_type=MESH)

    mine = yh * 4 + z
    th = ((td + 1) // 2) % 2

    def a_first(s):
        for i in range(2):
            push(remote(amp64.at[:, columns(s)], tbuf.at[mine, :, columns(s)],
                        a_s.at[s * 2 + i], a_r.at[s, trel * 4],
                        a_targets[i]))

    def a_slot(e, dz, s):
        return tbuf.at[((yh + e) % 2) * 4 + (z - dz + 4) % 4, :, columns(s)]

    def a_send(e, dz, s, sz):
        where = a_slot(e, dz, s)
        n = 6 + s * 6 + (e * 2 + sz // 2 if dz == 0 else 4 + e)
        push(remote(where, where, a_s.at[n], a_r.at[s, e * 4 + (dz + sz) % 4], plane(0, sz)))

    def a_wait(e, dz, s):
        where = a_slot(e, dz, s)
        remote(where, where, a_s.at[0], a_r.at[s, e * 4 + dz], sibling).wait_recv()

    def b_slot(dx, dz):
        do = (x - dx - q + 8) % 4
        return tbuf.at[((yh + do // 2) % 2) * 4 + (z - dz + 4) % 4, :, columns(3 + ((do + 1) // 2) % 2)]

    def b_send(n, dx, dz, sx, sz):
        where = b_slot(dx, dz)
        push(remote(where, where, b_s.at[n], b_r.at[((dx + sx) % 4) * 4 + (dz + sz) % 4], plane(sx, sz)))

    def b_wait(dx, dz):
        where = b_slot(dx, dz)
        remote(where, where, b_s.at[0], b_r.at[dx * 4 + dz], sibling).wait_recv()

    push(remote(amp64.at[:, columns(3 + th)], tbuf.at[mine, :, columns(3 + th)],
                b_s.at[0], b_r.at[0], b_target))
    a_first(0)
    a_first(1)
    a_first(2)
    for i in range(CH):
        for kind, to in ((0, other), (1, sibling)):
            push(pan_copy(kind, i, g, to))

    def a_step(s):
        for e in range(2):
            a_wait(e, 0, s)
            a_send(e, 0, s, 1)
            a_send(e, 0, s, 3)

    def a_pass(s):
        a_wait(0, 1, s)
        a_send(0, 1, s, 1)
        a_wait(1, 3, s)
        a_send(1, 3, s, 3)

    def b_step(dz):
        if dz:
            b_wait(0, dz)
        b_send(4 + dz * 2, 0, dz, 1, 0)
        b_send(5 + dz * 2, 0, dz, 3, 0)

    def expand(owner, i, put):
        b = lane + (owner * QR + i * 128)
        w = of_row(b, win).astype(F32)
        w = jnp.where(lane + i * 128 < QR, w, -1.0).astype(BF16)
        at = [w == jnp.asarray(v, BF16) for v in range(NW)]

        def rows(u, _):
            row = pl.multiple_of(u * 16, 16)
            part = [ctb[owner, i, pl.ds(pl.multiple_of(j * 128 + row, 16), 16), :] for j in range(WIN // 128)]
            for k in range(N // 128):
                acc = jnp.zeros((16, 128), BF16)
                for j in range(WIN // 128):
                    if 0 <= k - j < NW:
                        acc = jnp.where(at[k - j], part[j], acc)
                put(pl.ds(pl.multiple_of(k * 128 + row, 16), 16), acc)
            return 0

        lax.fori_loop(0, 8, rows, 0)

    def expand_to(owner, slot, i):
        def put(rows, value):
            mfull[rows, pl.ds(pl.multiple_of(slot * 512 + i * 128, 128), 128)] = value
        expand(owner, i, put)

    def b_pass(dz, dx):
        b_wait(dx, dz)
        b_send(12 + dz, dx, dz, dx, 0)

    def pass_on(i):
        pan_copy(0, i, far0 + c, sibling).wait_recv()
        push(pan_copy(2, i, far0 + c, sibling))

    def far_ready(i):
        pan_copy(2, i, far0 + 1 - c, sibling).wait_recv()

    def b_pass(dz, dx):
        b_wait(dx, dz)
        b_send(12 + dz, dx, dz, dx, 0)

    def rows_of(at, width):
        return tbuf[:, :, pl.ds(at, width)].reshape(8 * PAD, width)

    def expand_own(owner, slot):
        def body(i, _):
            expand_to(owner, slot, i)
            return 0

        lax.fori_loop(0, CH, body, 0)

    def expand_far(lo, hi, owner, slot):
        def body(i, _):
            widen(owner, i)
            expand_to(owner, slot, i)
            return 0

        lax.fori_loop(lo, hi, body, 0)

    near, far, last = yl * 2 + 1 - c, far0 + c, far0 + 1 - c
    expand_own(g, c)
    b_wait(0, 0)
    for n, sz in ((1, 1), (2, 3), (3, 2)):
        b_send(n, 0, 0, 0, sz)
    b_step(0)
    a_step(0)
    a_step(1)
    b_step(1)
    b_step(3)
    for i in range(CH):
        pan_copy(1, i, near, sibling).wait_recv()
    expand_own(near, 1 - c)
    pass_on(0)
    b_step(2)
    a_step(2)
    a_pass(0)
    b_pass(0, 1)
    b_pass(3, 3)
    pass_on(1)
    expand_far(0, 2, far, 2 + c)
    b_pass(1, 1)
    b_pass(2, 3)
    pass_on(2)
    a_pass(1)
    a_pass(2)
    pass_on(3)
    expand_far(2, 4, far, 2 + c)
    for i in range(CH):
        far_ready(i)
    expand_far(0, 4, last, 3 - c)
    for copy in fcopies:
        copy.wait()
    for dx in (1, 2, 3):
        for dz in range(4):
            if (dz, dx) not in ((0, 1), (3, 3), (1, 1), (2, 3)):
                b_wait(dx, dz)
    for s in range(3):
        for e, dz in ((0, 2), (0, 3), (1, 1), (1, 2)):
            a_wait(e, dz, s)

    rows_t = tbuf[...].reshape(8 * PAD, N)
    for col in range(0, 2048, 512):
        coupled[:, pl.ds(col, 512)] = jnp.dot(
            rows_t, mfull[:, pl.ds(col, 512)], preferred_element_type=F32).astype(BF16)
    for col, width in SPLIT:
        acc = jnp.dot(coupled[...], fall[:, pl.ds(col, width)], preferred_element_type=F32)
        for k in range(8):
            out[pl.ds(k * ROWS, ROWS), pl.ds(col, width)] = acc[k * PAD:k * PAD + ROWS].astype(BF16)
    for copy in pending:
        copy.wait_send()


def local(amplitudes, hole_panel, virt_fock, irrep_sizes, pair_irreps):
    wt = jnp.transpose(hole_panel.reshape(N, QR))
    vmem = pl.BlockSpec(memory_space=pltpu.VMEM)
    smem = pl.BlockSpec(memory_space=pltpu.SMEM)
    out = pl.pallas_call(
        kernel,
        out_shape=jax.ShapeDtypeStruct((QR, N), BF16),
        in_specs=[vmem, vmem, pl.BlockSpec(memory_space=pl.ANY), smem, smem],
        out_specs=vmem,
        scratch_shapes=[
            pltpu.VMEM((PAD, N), BF16),
            pltpu.VMEM((8, PAD, N), BF16),
            pltpu.VMEM((512, WIN), BF16),
            pltpu.VMEM((NG, CH, WIN, 128), BF16),
            pltpu.VMEM((NG, CH, FWIN, 128), BF16),
            pltpu.VMEM((N, 2048), BF16),
            pltpu.VMEM((2048, N), BF16),
            pltpu.VMEM((8 * PAD, 2048), BF16),
            pltpu.SemaphoreType.DMA((24,)),
            pltpu.SemaphoreType.DMA((3, 8)),
            pltpu.SemaphoreType.DMA((16,)),
            pltpu.SemaphoreType.DMA((16,)),
            pltpu.SemaphoreType.DMA((3, CH)),
            pltpu.SemaphoreType.DMA((3, CH)),
            pltpu.SemaphoreType.DMA((4,)),
        ],
        compiler_params=pltpu.CompilerParams(
            collective_id=0, has_side_effects=True, vmem_limit_bytes=60 << 20),
    )(amplitudes, wt, virt_fock, irrep_sizes, pair_irreps)
    return out.reshape(QR, 1, N)


def solution(mesh):
    in_specs = (P("blk", None), P(None, "blk", "grp"), P(), P(), P("blk"))
    out_specs = P("grp", "blk", None)
    return jax.shard_map(local, mesh=mesh, in_specs=in_specs, out_specs=out_specs, check_vma=False)
```

```python
import functools

import jax
import jax.numpy as jnp
from jax import lax
from jax.experimental import pallas as pl
from jax.experimental.pallas import tpu as pltpu
from jax.sharding import PartitionSpec as P

MESH = pl.DeviceIdType.MESH
F32, BF16 = jnp.float32, jnp.bfloat16
N = 1920
QR = 480
NB, NG = 32, 4
ROWS = 60
PAD = 64
WIN = 640
NW = (N - WIN) // 128 + 1
FWIN = 496
NF = (WIN - FWIN) // 16 + 1
SPLIT = ((0, 1024), (1024, 896))
CC = 384
CH = 4


def kernel(amp, wt, fock, sizes, pair, out,
           amp64, tbuf, cbuf, ctb, cts, mfull, fall, rows_t, coupled,
           a_s, a_r, b_s, b_r, pan_s, pan_r, f_sem):
    blk, g = lax.axis_index("blk"), lax.axis_index("grp")
    x, yh, z = blk // 8, (blk // 4) % 2, blk % 4
    yl, c = g // 2, g % 2

    def dev(x_, yh_, z_, yl_, c_):
        return (x_ * 8 + yh_ * 4 + z_, yl_ * 2 + c_)

    q = g
    d = (x - q + 4) % 4
    a_use = ((d + 3) % 4) // 2
    a_core = (a_use + c) % 2
    b_rel = d // 2
    b_core = (1 - b_rel) * ((c + 1 + d) % 2) + b_rel * ((d + 2) % 4)
    sources = [dev(q, yh, z, yl, a_core), dev(q, 1 - yh, z, 1 - yl, a_use),
               dev(q, (yh + b_rel) % 2, z, (yl + b_rel) % 2, b_core)]
    tyl, tc = x // 2, x % 2
    trel = (yl + tyl) % 2
    use = (1 - trel) * ((c + tc) % 2) + trel * c
    a_targets = [dev((x + 1 + 2 * use + i) % 4, (yh + trel) % 2, z, tyl, tc) for i in range(2)]
    td = (1 - trel) * (1 - (c + tc) % 2) + trel * (2 + c)
    b_target = dev((x + td) % 4, (yh + trel) % 2, z, tyl, tc)
    sibling = dev(x, yh, z, yl, 1 - c)
    other = dev(x, yh, z, 1 - yl, c)

    def plane(sx, sz):
        return dev((x + sx) % 4, yh, (z + sz) % 4, yl, c)

    bar = pltpu.get_barrier_semaphore()
    peers = [plane(s, 0) for s in (1, 2, 3)] + [plane(0, s) for s in (1, 2, 3)]
    for to in peers + sources + [sibling, other]:
        pl.semaphore_signal(bar, inc=1, device_id=to, device_id_type=MESH)
    far0 = (1 - yl) * 2
    fcopies = []
    for slot in range(4):
        owner = (yl * 2 + slot) % 4
        fcopies.append(pltpu.make_async_copy(
            fock.at[pl.ds(pl.multiple_of(owner * QR, 16), QR)],
            fall.at[pl.ds(slot * 512, QR)], f_sem.at[slot]))
    for copy in fcopies:
        copy.start()
    for slot in range(4):
        fall[pl.ds(slot * 512 + QR, 32), :] = jnp.zeros((32, N), BF16)
    amp64[pl.ds(0, ROWS), :] = amp[...]
    amp64[pl.ds(ROWS, PAD - ROWS), :] = jnp.zeros((PAD - ROWS, N), BF16)

    p = pair[0]
    run = jnp.int32(0)
    bound = []
    for r in range(8):
        bound.append(run)
        run = run + sizes[r]
    bound.append(run)
    lo, hi, win = [], [], []
    for r in range(8):
        s = jnp.bitwise_xor(jnp.int32(r), p)
        first_lane, end_lane = jnp.int32(0), jnp.int32(0)
        for i in range(8):
            first_lane = jnp.where(s == i, bound[i], first_lane)
            end_lane = jnp.where(s == i, bound[i + 1], end_lane)
        lo.append(first_lane)
        hi.append(end_lane)
        win.append(jnp.minimum(jnp.right_shift(first_lane, 7), NW - 1))
    fine = [jnp.minimum(jnp.right_shift(lo[r], 4), (N - FWIN) // 16) - win[r] * 8 for r in range(8)]
    left_of = [lo[r] - win[r] * 128 for r in range(8)]
    right_of = [hi[r] - win[r] * 128 for r in range(8)]

    base = g * QR

    def pan_copy(kind, i, owner, to):
        part = (cts if kind == 0 else ctb).at[owner, i]
        return pltpu.make_async_remote_copy(
            part, part, pan_s.at[kind, i], pan_r.at[kind, i], device_id=to, device_id_type=MESH)

    lane = lax.broadcasted_iota(jnp.int32, (16, 128), 1)
    sub = lax.broadcasted_iota(jnp.int32, (16, 128), 0)

    def of_row(b, values):
        pick = jnp.full((16, 128), values[0])
        for r in range(1, 8):
            pick = jnp.where(b >= bound[r], values[r], pick)
        return pick

    def masks(b):
        w = of_row(b, win).astype(F32).astype(BF16)
        return [w == jnp.asarray(v, BF16) for v in range(NW)]

    def compact(t, _):
        row = pl.multiple_of(t * 16, 16)
        b = sub + (base + row)
        at = masks(b)
        left, right = of_row(b, left_of), of_row(b, right_of)
        for j in range(WIN // 128):
            acc = wt[pl.ds(row, 16), pl.ds(j * 128, 128)]
            for v in range(1, NW):
                acc = jnp.where(at[v], wt[pl.ds(row, 16), pl.ds((v + j) * 128, 128)], acc)
            keep = (lane + j * 128 >= left) & (lane + j * 128 < right)
            acc = jnp.where(keep, acc.astype(F32), 0.0).astype(BF16)
            cbuf[pl.ds(row, 16), pl.ds(j * 128, 128)] = acc
        return 0

    lax.fori_loop(0, QR // 16, compact, 0)
    cbuf[pl.ds(QR, 32), :] = jnp.zeros((32, WIN), BF16)
    for i in range(CH):
        ctb[g, i] = jnp.transpose(cbuf[pl.ds(i * 128, 128), :])

    def fine_masks(owner, i):
        f = of_row(lane + (owner * QR + i * 128), fine).astype(F32).astype(BF16)
        return [f == jnp.asarray(v, BF16) for v in range(NF)]

    def narrow(i, _):
        at = fine_masks(g, i)
        for u in range(FWIN // 16):
            acc = ctb[g, i, pl.ds(u * 16, 16), :]
            for v in range(1, NF):
                acc = jnp.where(at[v], ctb[g, i, pl.ds((u + v) * 16, 16), :], acc)
            cts[g, i, pl.ds(u * 16, 16), :] = acc
        return 0

    def widen(owner, i):
        at = fine_masks(owner, i)
        for u in range(WIN // 16):
            acc = jnp.zeros((16, 128), BF16)
            for v in range(NF):
                if 0 <= u - v < FWIN // 16:
                    acc = jnp.where(at[v], cts[owner, i, pl.ds((u - v) * 16, 16), :], acc)
            ctb[owner, i, pl.ds(u * 16, 16), :] = acc

    lax.fori_loop(0, CH, narrow, 0)
    pl.semaphore_wait(bar, len(peers) + 5)

    pending = []

    def push(copy):
        copy.start()
        pending.append(copy)

    def columns(chunk):
        return pl.ds(pl.multiple_of(chunk * CC, 128), CC)

    def remote(src, dst, s_sem, r_sem, to):
        return pltpu.make_async_remote_copy(src, dst, s_sem, r_sem, device_id=to, device_id_type=MESH)

    mine = yh * 4 + z
    th = ((td + 1) // 2) % 2

    def a_first(s):
        for i in range(2):
            push(remote(amp64.at[:, columns(s)], tbuf.at[mine, :, columns(s)],
                        a_s.at[s * 2 + i], a_r.at[s, trel * 4],
                        a_targets[i]))

    def a_slot(e, dz, s):
        return tbuf.at[((yh + e) % 2) * 4 + (z - dz + 4) % 4, :, columns(s)]

    def a_send(e, dz, s, sz):
        where = a_slot(e, dz, s)
        n = 6 + s * 6 + (e * 2 + sz // 2 if dz == 0 else 4 + e)
        push(remote(where, where, a_s.at[n], a_r.at[s, e * 4 + (dz + sz) % 4], plane(0, sz)))

    def a_wait(e, dz, s):
        where = a_slot(e, dz, s)
        remote(where, where, a_s.at[0], a_r.at[s, e * 4 + dz], sibling).wait_recv()

    def b_slot(dx, dz):
        do = (x - dx - q + 8) % 4
        return tbuf.at[((yh + do // 2) % 2) * 4 + (z - dz + 4) % 4, :, columns(3 + ((do + 1) // 2) % 2)]

    def b_send(n, dx, dz, sx, sz):
        where = b_slot(dx, dz)
        push(remote(where, where, b_s.at[n], b_r.at[((dx + sx) % 4) * 4 + (dz + sz) % 4], plane(sx, sz)))

    def b_wait(dx, dz):
        where = b_slot(dx, dz)
        remote(where, where, b_s.at[0], b_r.at[dx * 4 + dz], sibling).wait_recv()

    push(remote(amp64.at[:, columns(3 + th)], tbuf.at[mine, :, columns(3 + th)],
                b_s.at[0], b_r.at[0], b_target))
    a_first(0)
    a_first(1)
    a_first(2)
    for i in range(CH):
        for kind, to in ((0, other), (1, sibling)):
            push(pan_copy(kind, i, g, to))

    def a_step(s):
        for e in range(2):
            a_wait(e, 0, s)
            a_send(e, 0, s, 1)
            a_send(e, 0, s, 3)

    def a_pass(s):
        a_wait(0, 1, s)
        a_send(0, 1, s, 1)
        a_wait(1, 3, s)
        a_send(1, 3, s, 3)

    def b_step(dz):
        if dz:
            b_wait(0, dz)
        b_send(4 + dz * 2, 0, dz, 1, 0)
        b_send(5 + dz * 2, 0, dz, 3, 0)
        b_send(12 + dz, 0, dz, 2, 0)

    def expand(owner, i, put):
        b = lane + (owner * QR + i * 128)
        w = of_row(b, win).astype(F32)
        w = jnp.where(lane + i * 128 < QR, w, -1.0).astype(BF16)
        at = [w == jnp.asarray(v, BF16) for v in range(NW)]

        def rows(u, _):
            row = pl.multiple_of(u * 16, 16)
            part = [ctb[owner, i, pl.ds(pl.multiple_of(j * 128 + row, 16), 16), :] for j in range(WIN // 128)]
            for k in range(N // 128):
                acc = jnp.zeros((16, 128), BF16)
                for j in range(WIN // 128):
                    if 0 <= k - j < NW:
                        acc = jnp.where(at[k - j], part[j], acc)
                put(pl.ds(pl.multiple_of(k * 128 + row, 16), 16), acc)
            return 0

        lax.fori_loop(0, 8, rows, 0)

    def expand_to(owner, slot, i):
        def put(rows, value):
            mfull[rows, pl.ds(pl.multiple_of(slot * 512 + i * 128, 128), 128)] = value
        expand(owner, i, put)

    def pass_on(i):
        pan_copy(0, i, far, sibling).wait_recv()
        widen(far, i)
        push(pan_copy(2, i, far, sibling))

    def far_ready(i):
        pan_copy(2, i, far0 + 1 - c, sibling).wait_recv()

    def b_pass(dz, dx):
        b_wait(dx, dz)
        b_send(12 + dz, dx, dz, dx, 0)

    def rows_of(at, width):
        return tbuf[:, :, pl.ds(at, width)].reshape(8 * PAD, width)

    def expand_some(owner, slot, lo, hi):
        def body(i, _):
            expand_to(owner, slot, i)
            return 0

        lax.fori_loop(lo, hi, body, 0)

    near, far, last = yl * 2 + 1 - c, far0 + c, far0 + 1 - c
    expand_some(g, c, 0, CH)
    b_wait(0, 0)
    for n, sz in ((1, 1), (2, 3), (3, 2)):
        b_send(n, 0, 0, 0, sz)
    b_step(0)
    a_step(0)
    a_step(1)
    b_step(1)
    b_step(3)
    for i in range(CH):
        pan_copy(1, i, near, sibling).wait_recv()
    expand_some(near, 1 - c, 0, CH)
    b_step(2)
    a_step(2)
    pass_on(0)
    a_pass(0)
    pass_on(1)
    expand_some(far, 2 + c, 0, 2)
    a_pass(1)
    pass_on(2)
    a_pass(2)
    pass_on(3)
    expand_some(far, 2 + c, 2, CH)
    for i in range(CH):
        far_ready(i)
    expand_some(last, 3 - c, 0, CH)
    for copy in fcopies:
        copy.wait()
    for copy in pending:
        copy.wait_send()
    for dx in (1, 2, 3):
        for dz in range(4):
            b_wait(dx, dz)
    for s in range(3):
        for e, dz in ((0, 2), (0, 3), (1, 1), (1, 2)):
            a_wait(e, dz, s)

    for k in range(8):
        rows_t[pl.ds(k * ROWS, ROWS), :] = tbuf[k, pl.ds(0, ROWS), :]
    for col in range(0, 2048, 1024):
        coupled[:, pl.ds(col, 1024)] = jnp.dot(
            rows_t[...], mfull[:, pl.ds(col, 1024)], preferred_element_type=F32).astype(BF16)
    for col, width in SPLIT:
        out[:, pl.ds(col, width)] = jnp.dot(
            coupled[...], fall[:, pl.ds(col, width)], preferred_element_type=F32).astype(BF16)


def local(amplitudes, hole_panel, virt_fock, irrep_sizes, pair_irreps):
    wt = jnp.transpose(hole_panel.reshape(N, QR))
    vmem = pl.BlockSpec(memory_space=pltpu.VMEM)
    smem = pl.BlockSpec(memory_space=pltpu.SMEM)
    out = pl.pallas_call(
        kernel,
        out_shape=jax.ShapeDtypeStruct((QR, N), BF16),
        in_specs=[vmem, vmem, pl.BlockSpec(memory_space=pl.ANY), smem, smem],
        out_specs=vmem,
        scratch_shapes=[
            pltpu.VMEM((PAD, N), BF16),
            pltpu.VMEM((8, PAD, N), BF16),
            pltpu.VMEM((512, WIN), BF16),
            pltpu.VMEM((NG, CH, WIN, 128), BF16),
            pltpu.VMEM((NG, CH, FWIN, 128), BF16),
            pltpu.VMEM((N, 2048), BF16),
            pltpu.VMEM((2048, N), BF16),
            pltpu.VMEM((QR, N), BF16),
            pltpu.VMEM((QR, 2048), BF16),
            pltpu.SemaphoreType.DMA((24,)),
            pltpu.SemaphoreType.DMA((3, 8)),
            pltpu.SemaphoreType.DMA((16,)),
            pltpu.SemaphoreType.DMA((16,)),
            pltpu.SemaphoreType.DMA((3, CH)),
            pltpu.SemaphoreType.DMA((3, CH)),
            pltpu.SemaphoreType.DMA((4,)),
        ],
        compiler_params=pltpu.CompilerParams(
            collective_id=0, has_side_effects=True, vmem_limit_bytes=60 << 20),
    )(amplitudes, wt, virt_fock, irrep_sizes, pair_irreps)
    return out.reshape(QR, 1, N)


def solution(mesh):
    in_specs = (P("blk", None), P(None, "blk", "grp"), P(), P(), P("blk"))
    out_specs = P("grp", "blk", None)
    return jax.shard_map(local, mesh=mesh, in_specs=in_specs, out_specs=out_specs, check_vma=False)
```

```python
import functools

import jax
import jax.numpy as jnp
from jax import lax
from jax.experimental import pallas as pl
from jax.experimental.pallas import tpu as pltpu
from jax.sharding import PartitionSpec as P

MESH = pl.DeviceIdType.MESH
F32, BF16 = jnp.float32, jnp.bfloat16
N = 1920
QR = 480
NB, NG = 32, 4
ROWS = 60
PAD = 64
WIN = 640
NW = (N - WIN) // 128 + 1
FWIN = 496
NF = (WIN - FWIN) // 16 + 1
SPLIT = ((0, 1024), (1024, 896))
CC = 384
CH = 4


def kernel(amp, wt, fock, sizes, pair, out,
           amp64, tbuf, cbuf, ctb, cts, mfull, fall, rows_t, coupled,
           a_s, a_r, b_s, b_r, pan_s, pan_r, f_sem):
    blk, g = lax.axis_index("blk"), lax.axis_index("grp")
    x, yh, z = blk // 8, (blk // 4) % 2, blk % 4
    yl, c = g // 2, g % 2

    def dev(x_, yh_, z_, yl_, c_):
        return (x_ * 8 + yh_ * 4 + z_, yl_ * 2 + c_)

    q = g
    d = (x - q + 4) % 4
    a_use = ((d + 3) % 4) // 2
    a_core = (a_use + c) % 2
    b_rel = d // 2
    b_core = (1 - b_rel) * ((c + 1 + d) % 2) + b_rel * ((d + 2) % 4)
    sources = [dev(q, yh, z, yl, a_core), dev(q, 1 - yh, z, 1 - yl, a_use),
               dev(q, (yh + b_rel) % 2, z, (yl + b_rel) % 2, b_core)]
    tyl, tc = x // 2, x % 2
    trel = (yl + tyl) % 2
    use = (1 - trel) * ((c + tc) % 2) + trel * c
    a_targets = [dev((x + 1 + 2 * use + i) % 4, (yh + trel) % 2, z, tyl, tc) for i in range(2)]
    td = (1 - trel) * (1 - (c + tc) % 2) + trel * (2 + c)
    b_target = dev((x + td) % 4, (yh + trel) % 2, z, tyl, tc)
    sibling = dev(x, yh, z, yl, 1 - c)
    other = dev(x, yh, z, 1 - yl, c)

    def plane(sx, sz):
        return dev((x + sx) % 4, yh, (z + sz) % 4, yl, c)

    bar = pltpu.get_barrier_semaphore()
    peers = [plane(s, 0) for s in (1, 2, 3)] + [plane(0, s) for s in (1, 2, 3)]
    for to in peers + sources + [sibling, other]:
        pl.semaphore_signal(bar, inc=1, device_id=to, device_id_type=MESH)
    far0 = (1 - yl) * 2
    fcopies = []
    for slot in range(4):
        owner = (yl * 2 + slot) % 4
        fcopies.append(pltpu.make_async_copy(
            fock.at[pl.ds(pl.multiple_of(owner * QR, 16), QR)],
            fall.at[pl.ds(slot * 512, QR)], f_sem.at[slot]))
    for copy in fcopies:
        copy.start()
    for slot in range(4):
        fall[pl.ds(slot * 512 + QR, 32), :] = jnp.zeros((32, N), BF16)
    amp64[pl.ds(0, ROWS), :] = amp[...]
    amp64[pl.ds(ROWS, PAD - ROWS), :] = jnp.zeros((PAD - ROWS, N), BF16)

    p = pair[0]
    run = jnp.int32(0)
    bound = []
    for r in range(8):
        bound.append(run)
        run = run + sizes[r]
    bound.append(run)
    lo, hi, win = [], [], []
    for r in range(8):
        s = jnp.bitwise_xor(jnp.int32(r), p)
        first_lane, end_lane = jnp.int32(0), jnp.int32(0)
        for i in range(8):
            first_lane = jnp.where(s == i, bound[i], first_lane)
            end_lane = jnp.where(s == i, bound[i + 1], end_lane)
        lo.append(first_lane)
        hi.append(end_lane)
        win.append(jnp.minimum(jnp.right_shift(first_lane, 7), NW - 1))
    fine = [jnp.minimum(jnp.right_shift(lo[r], 4), (N - FWIN) // 16) - win[r] * 8 for r in range(8)]
    left_of = [lo[r] - win[r] * 128 for r in range(8)]
    right_of = [hi[r] - win[r] * 128 for r in range(8)]

    base = g * QR

    def pan_copy(kind, i, owner, to):
        part = (cts if kind == 0 else ctb).at[owner, i]
        return pltpu.make_async_remote_copy(
            part, part, pan_s.at[kind, i], pan_r.at[kind, i], device_id=to, device_id_type=MESH)

    lane = lax.broadcasted_iota(jnp.int32, (16, 128), 1)
    sub = lax.broadcasted_iota(jnp.int32, (16, 128), 0)

    def of_row(b, values):
        pick = jnp.full((16, 128), values[0])
        for r in range(1, 8):
            pick = jnp.where(b >= bound[r], values[r], pick)
        return pick

    def masks(b):
        w = of_row(b, win).astype(F32).astype(BF16)
        return [w == jnp.asarray(v, BF16) for v in range(NW)]

    def compact(t, _):
        row = pl.multiple_of(t * 16, 16)
        b = sub + (base + row)
        at = masks(b)
        left, right = of_row(b, left_of), of_row(b, right_of)
        for j in range(WIN // 128):
            acc = wt[pl.ds(row, 16), pl.ds(j * 128, 128)]
            for v in range(1, NW):
                acc = jnp.where(at[v], wt[pl.ds(row, 16), pl.ds((v + j) * 128, 128)], acc)
            keep = (lane + j * 128 >= left) & (lane + j * 128 < right)
            acc = jnp.where(keep, acc.astype(F32), 0.0).astype(BF16)
            cbuf[pl.ds(row, 16), pl.ds(j * 128, 128)] = acc
        return 0

    lax.fori_loop(0, QR // 16, compact, 0)
    cbuf[pl.ds(QR, 32), :] = jnp.zeros((32, WIN), BF16)
    for i in range(CH):
        ctb[g, i] = jnp.transpose(cbuf[pl.ds(i * 128, 128), :])

    def fine_masks(owner, i):
        f = of_row(lane + (owner * QR + i * 128), fine).astype(F32).astype(BF16)
        return [f == jnp.asarray(v, BF16) for v in range(NF)]

    def narrow(i, _):
        at = fine_masks(g, i)
        for u in range(FWIN // 16):
            acc = ctb[g, i, pl.ds(u * 16, 16), :]
            for v in range(1, NF):
                acc = jnp.where(at[v], ctb[g, i, pl.ds((u + v) * 16, 16), :], acc)
            cts[g, i, pl.ds(u * 16, 16), :] = acc
        return 0

    def widen(owner, i):
        at = fine_masks(owner, i)
        for u in range(WIN // 16):
            acc = jnp.zeros((16, 128), BF16)
            for v in range(NF):
                if 0 <= u - v < FWIN // 16:
                    acc = jnp.where(at[v], cts[owner, i, pl.ds((u - v) * 16, 16), :], acc)
            ctb[owner, i, pl.ds(u * 16, 16), :] = acc

    lax.fori_loop(0, CH, narrow, 0)
    pl.semaphore_wait(bar, len(peers) + 5)

    pending = []

    def push(copy):
        copy.start()
        pending.append(copy)

    def columns(chunk):
        return pl.ds(pl.multiple_of(chunk * CC, 128), CC)

    def remote(src, dst, s_sem, r_sem, to):
        return pltpu.make_async_remote_copy(src, dst, s_sem, r_sem, device_id=to, device_id_type=MESH)

    mine = yh * 4 + z
    th = ((td + 1) // 2) % 2

    def a_first(s):
        for i in range(2):
            push(remote(amp64.at[:, columns(s)], tbuf.at[mine, :, columns(s)],
                        a_s.at[s * 2 + i], a_r.at[s, trel * 4],
                        a_targets[i]))

    def a_slot(e, dz, s):
        return tbuf.at[((yh + e) % 2) * 4 + (z - dz + 4) % 4, :, columns(s)]

    def a_send(e, dz, s, sz):
        where = a_slot(e, dz, s)
        n = 6 + s * 6 + (e * 2 + sz // 2 if dz == 0 else 4 + e)
        push(remote(where, where, a_s.at[n], a_r.at[s, e * 4 + (dz + sz) % 4], plane(0, sz)))

    def a_wait(e, dz, s):
        where = a_slot(e, dz, s)
        remote(where, where, a_s.at[0], a_r.at[s, e * 4 + dz], sibling).wait_recv()

    def b_slot(dx, dz):
        do = (x - dx - q + 8) % 4
        return tbuf.at[((yh + do // 2) % 2) * 4 + (z - dz + 4) % 4, :, columns(3 + ((do + 1) // 2) % 2)]

    def b_send(n, dx, dz, sx, sz):
        where = b_slot(dx, dz)
        push(remote(where, where, b_s.at[n], b_r.at[((dx + sx) % 4) * 4 + (dz + sz) % 4], plane(sx, sz)))

    def b_wait(dx, dz):
        where = b_slot(dx, dz)
        remote(where, where, b_s.at[0], b_r.at[dx * 4 + dz], sibling).wait_recv()

    push(remote(amp64.at[:, columns(3 + th)], tbuf.at[mine, :, columns(3 + th)],
                b_s.at[0], b_r.at[0], b_target))
    a_first(0)
    a_first(1)
    a_first(2)
    for i in range(CH):
        for kind, to in ((0, other), (1, sibling)):
            push(pan_copy(kind, i, g, to))

    def a_step(s):
        for e in range(2):
            a_wait(e, 0, s)
            a_send(e, 0, s, 1)
            a_send(e, 0, s, 3)

    def a_pass(s):
        a_wait(0, 1, s)
        a_send(0, 1, s, 1)
        a_wait(1, 3, s)
        a_send(1, 3, s, 3)

    def b_step(dz):
        if dz:
            b_wait(0, dz)
        b_send(4 + dz * 2, 0, dz, 1, 0)
        b_send(5 + dz * 2, 0, dz, 3, 0)
        b_send(12 + dz, 0, dz, 2, 0)

    def expand(owner, i, put):
        b = lane + (owner * QR + i * 128)
        w = of_row(b, win).astype(F32)
        w = jnp.where(lane + i * 128 < QR, w, -1.0).astype(BF16)
        at = [w == jnp.asarray(v, BF16) for v in range(NW)]

        def rows(u, _):
            row = pl.multiple_of(u * 16, 16)
            part = [ctb[owner, i, pl.ds(pl.multiple_of(j * 128 + row, 16), 16), :] for j in range(WIN // 128)]
            for k in range(N // 128):
                acc = jnp.zeros((16, 128), BF16)
                for j in range(WIN // 128):
                    if 0 <= k - j < NW:
                        acc = jnp.where(at[k - j], part[j], acc)
                put(pl.ds(pl.multiple_of(k * 128 + row, 16), 16), acc)
            return 0

        lax.fori_loop(0, 8, rows, 0)

    def expand_to(owner, slot, i):
        def put(rows, value):
            mfull[rows, pl.ds(pl.multiple_of(slot * 512 + i * 128, 128), 128)] = value
        expand(owner, i, put)

    def pass_on(i):
        pan_copy(0, i, far, sibling).wait_recv()
        widen(far, i)
        push(pan_copy(2, i, far, sibling))

    def far_ready(i):
        pan_copy(2, i, far0 + 1 - c, sibling).wait_recv()

    def b_pass(dz, dx):
        b_wait(dx, dz)
        b_send(12 + dz, dx, dz, dx, 0)

    def rows_of(at, width):
        return tbuf[:, :, pl.ds(at, width)].reshape(8 * PAD, width)

    def expand_some(owner, slot, lo, hi):
        def body(i, _):
            expand_to(owner, slot, i)
            return 0

        lax.fori_loop(lo, hi, body, 0)

    near, far, last = yl * 2 + 1 - c, far0 + c, far0 + 1 - c
    expand_some(g, c, 0, CH)
    b_wait(0, 0)
    for n, sz in ((1, 1), (2, 3), (3, 2)):
        b_send(n, 0, 0, 0, sz)
    b_step(0)
    a_step(0)
    a_step(1)
    b_step(1)
    b_step(3)
    for i in range(CH):
        pan_copy(1, i, near, sibling).wait_recv()
    expand_some(near, 1 - c, 0, CH)
    b_step(2)
    a_step(2)
    pass_on(0)
    a_pass(0)
    pass_on(1)
    expand_some(far, 2 + c, 0, 2)
    a_pass(1)
    pass_on(2)
    a_pass(2)
    pass_on(3)
    expand_some(far, 2 + c, 2, CH)
    for i in range(CH):
        far_ready(i)
    expand_some(last, 3 - c, 0, CH)
    for copy in fcopies:
        copy.wait()
    for copy in pending:
        copy.wait_send()
    for dx in (1, 2, 3):
        for dz in range(4):
            b_wait(dx, dz)
    for k in range(8):
        rows_t[pl.ds(k * ROWS, ROWS), pl.ds(3 * CC, 2 * CC)] = tbuf[k, pl.ds(0, ROWS), pl.ds(3 * CC, 2 * CC)]
    for s in range(3):
        for e, dz in ((0, 2), (0, 3), (1, 1), (1, 2)):
            a_wait(e, dz, s)

    for k in range(8):
        rows_t[pl.ds(k * ROWS, ROWS), pl.ds(0, 3 * CC)] = tbuf[k, pl.ds(0, ROWS), pl.ds(0, 3 * CC)]
    for col in range(0, 2048, 1024):
        coupled[:, pl.ds(col, 1024)] = jnp.dot(
            rows_t[...], mfull[:, pl.ds(col, 1024)], preferred_element_type=F32).astype(BF16)
    for col, width in SPLIT:
        out[:, pl.ds(col, width)] = jnp.dot(
            coupled[...], fall[:, pl.ds(col, width)], preferred_element_type=F32).astype(BF16)


def local(amplitudes, hole_panel, virt_fock, irrep_sizes, pair_irreps):
    wt = jnp.transpose(hole_panel.reshape(N, QR))
    vmem = pl.BlockSpec(memory_space=pltpu.VMEM)
    smem = pl.BlockSpec(memory_space=pltpu.SMEM)
    out = pl.pallas_call(
        kernel,
        out_shape=jax.ShapeDtypeStruct((QR, N), BF16),
        in_specs=[vmem, vmem, pl.BlockSpec(memory_space=pl.ANY), smem, smem],
        out_specs=vmem,
        scratch_shapes=[
            pltpu.VMEM((PAD, N), BF16),
            pltpu.VMEM((8, PAD, N), BF16),
            pltpu.VMEM((512, WIN), BF16),
            pltpu.VMEM((NG, CH, WIN, 128), BF16),
            pltpu.VMEM((NG, CH, FWIN, 128), BF16),
            pltpu.VMEM((N, 2048), BF16),
            pltpu.VMEM((2048, N), BF16),
            pltpu.VMEM((QR, N), BF16),
            pltpu.VMEM((QR, 2048), BF16),
            pltpu.SemaphoreType.DMA((24,)),
            pltpu.SemaphoreType.DMA((3, 8)),
            pltpu.SemaphoreType.DMA((16,)),
            pltpu.SemaphoreType.DMA((16,)),
            pltpu.SemaphoreType.DMA((3, CH)),
            pltpu.SemaphoreType.DMA((3, CH)),
            pltpu.SemaphoreType.DMA((4,)),
        ],
        compiler_params=pltpu.CompilerParams(
            collective_id=0, has_side_effects=True, vmem_limit_bytes=60 << 20),
    )(amplitudes, wt, virt_fock, irrep_sizes, pair_irreps)
    return out.reshape(QR, 1, N)


def solution(mesh):
    in_specs = (P("blk", None), P(None, "blk", "grp"), P(), P(), P("blk"))
    out_specs = P("grp", "blk", None)
    return jax.shard_map(local, mesh=mesh, in_specs=in_specs, out_specs=out_specs, check_vma=False)
```
